512 devices in a mesh: dp: 16 (over z_hi, x), expert: 32 (over z_lo, y, core).
Axes of the slice: x: 4, y: 8, z: 8 (z_hi: 4, z_lo: 2; z = z_hi * 2 + z_lo), core: 2. Of those that a mesh axis runs over, the one named last changes fastest.
Arguments:
- tokens: bfloat16 [6144, 6144], P('expert', 'dp'), may hold values from -6 to 6
- expert_of: int32 [6144], P('expert'), may hold values from 0 to 31, as said below
- router_weight: float32 [6144], P('expert'), may hold values from 0.2 to 1
- cotangent: bfloat16 [6144, 6144], P('expert', 'dp'), may hold values from -6 to 6
- gate_up_weight: bfloat16 [32, 2, 6144, 1024], P('expert', None, 'dp'), may hold values from -0.078125 to 0.078125
- down_weight: bfloat16 [32, 1024, 6144], P('expert', None, 'dp'), may hold values from -0.1875 to 0.1875
Outputs:
- layer_out: bfloat16 [6144, 6144], P('expert', 'dp')
- grad_tokens: bfloat16 [6144, 6144], P('expert', 'dp')
- grad_gate_up: bfloat16 [32, 2, 6144, 1024], P('expert', None, 'dp')
- grad_down: bfloat16 [32, 1024, 6144], P('expert', None, 'dp')
The draws below stay inside these ranges and needn't reach their ends.
Inputs may be any that keep to these rules, and one draw needn't show every extreme that they name: `expert_of`: take the tokens in aligned blocks of 192, one block for each index of expert. One expert, the same for all blocks, is named by exactly 12 tokens of every block; every other expert is named by at most 9 tokens of a block, and in every block some other expert by exactly 9.
All inputs are finite; a program needn't handle non-finite values.
Results may differ from the reference program's by a relative error of at most 0.0058.
Values may be sent and summed in bfloat16 or wider, within the bound.
No kernel may reach another device: no remote copies, remote signals or barrier semaphores. Data moves between devices by JAX's collectives and lax.ppermute only.
A program may use at most 64 MiB of HBM per device.

```python
import jax
import jax.numpy as jnp
from jax import lax

D = 6144
FF = 1024
TOK_DEV = 192
EXPERTS = 32
TOKENS = 6144
CAP_HOT = 12
CAP = 9


def draw_expert_of(key, part):
    hot_expert = jax.random.randint(jax.random.fold_in(key, 1), (), 0, EXPERTS).astype(jnp.int32)

    def one_block(block_key):
        first_key, second_key, third_key = jax.random.split(block_key, 3)
        order = jax.random.permutation(first_key, EXPERTS - 1).astype(jnp.int32)
        others = (hot_expert + 1 + order) % EXPERTS
        extra = jax.random.permutation(second_key, (EXPERTS - 2) * CAP)[:TOK_DEV - CAP_HOT - CAP]
        owner_rank = 1 + extra // CAP
        rank_counts = jnp.sum((owner_rank[:, None] == jnp.arange(EXPERTS - 1)[None, :]).astype(jnp.int32), axis=0)
        rank_counts = rank_counts.at[0].set(CAP)
        counts = jnp.zeros((EXPERTS,), jnp.int32).at[others].set(rank_counts).at[hot_expert].set(CAP_HOT)
        labels = jnp.repeat(jnp.arange(EXPERTS, dtype=jnp.int32), counts, total_repeat_length=TOK_DEV)
        return jax.random.permutation(third_key, labels)
    block_keys = jax.random.split(jax.random.fold_in(key, 2), EXPERTS)
    return jax.vmap(one_block)(block_keys).reshape(-1).astype(jnp.int32)


def level_of(stream_key, extent, cuts, low, top_value):
    loudness = 1.0
    for dim, shards_of in cuts:
        steps = jax.random.uniform(jax.random.fold_in(jax.random.fold_in(stream_key, 6), dim), (shards_of,), jnp.float32, low / len(cuts), top_value / len(cuts))
        loudness = loudness * jnp.repeat(jnp.exp(steps), extent[dim] // shards_of).reshape((-1,) + (1,) * (len(extent) - 1 - dim))
    return loudness


def noise(rng, dims, spread, limit, pieces=(), kind=jnp.bfloat16):
    factor_of = level_of(rng, dims, pieces, -0.22, 0.18) if pieces else 1.0
    drawn = jax.random.normal(rng, dims, jnp.float32) * spread * factor_of
    return jnp.minimum(jnp.maximum(drawn, -limit), limit).astype(kind)


def setup_inputs(seed: int = 0) -> dict:
    keys = jax.random.split(jax.random.key(seed), 7)
    tokens = noise(keys[0], (TOKENS, D), 1.0, 6.0, ((0, 32), (1, 16)))
    expert_of = draw_expert_of(jax.random.fold_in(keys[6], 71), 0)
    router_weight = jnp.clip(0.2 + 0.8 * jax.random.uniform(keys[2], (TOKENS,), jnp.float32) ** level_of(keys[2], (TOKENS,), ((0, 32),), -0.2, 0.2), 0.2, 1.0)
    cotangent = noise(keys[3], (TOKENS, D), 1.0, 6.0, ((0, 32), (1, 16)))
    gate_up_weight = noise(keys[4], (EXPERTS, 2, D, FF), D ** -0.5, 0.078125, ((0, 32), (2, 16)))
    down_weight = noise(keys[5], (EXPERTS, FF, D), FF ** -0.5, 0.1875, ((0, 32), (2, 16)))
    return dict(tokens=tokens, expert_of=expert_of, router_weight=router_weight, cotangent=cotangent, gate_up_weight=gate_up_weight, down_weight=down_weight)


def expert_math(inputs):
    token_index, is_valid, gate_up_slab, down_slab, tokens, scaled = inputs
    row_block = jnp.where(is_valid[:, None], tokens[token_index], jnp.zeros_like(tokens[token_index]))
    cot_rows = jnp.where(is_valid[:, None], scaled[token_index], jnp.zeros_like(scaled[token_index]))
    pre = jnp.einsum('rd,kdf->rkf', row_block.astype(jnp.float32), gate_up_slab.astype(jnp.float32))
    gate_value = pre[:, 0]
    up_value = pre[:, 1]
    sigmoid_gate = jax.nn.sigmoid(gate_value)
    activated = gate_value * sigmoid_gate
    hidden = (activated * up_value).astype(jnp.bfloat16)
    expert_out = jnp.dot(hidden, down_slab, preferred_element_type=jnp.float32).astype(jnp.bfloat16)
    hidden_grad = jnp.einsum('rd,fd->rf', cot_rows.astype(jnp.float32), down_slab.astype(jnp.float32))
    gate_grad = hidden_grad * up_value * sigmoid_gate * (1.0 + gate_value * (1.0 - sigmoid_gate))
    up_grad = hidden_grad * activated
    gate_up_grad = jnp.stack([gate_grad, up_grad], axis=1).astype(jnp.bfloat16)
    row_grad = jnp.einsum('rkf,kdf->rd', gate_up_grad.astype(jnp.float32), gate_up_slab.astype(jnp.float32)).astype(jnp.bfloat16)
    weight_grad = jnp.einsum('rd,rkf->kdf', row_block.astype(jnp.float32), gate_up_grad.astype(jnp.float32)).astype(jnp.bfloat16)
    down_grad = jnp.dot(hidden.T, cot_rows, preferred_element_type=jnp.float32).astype(jnp.bfloat16)
    return expert_out, row_grad, weight_grad, down_grad


def reference(tokens, expert_of, router_weight, cotangent, gate_up_weight, down_weight):
    token_total = tokens.shape[0]
    slot_total = EXPERTS * CAP_HOT
    onehot = (expert_of[:, None] == jnp.arange(EXPERTS, dtype=jnp.int32)[None, :]).astype(jnp.int32)
    position = jnp.sum((jnp.cumsum(onehot, axis=0) - onehot) * onehot, axis=1).astype(jnp.int32)
    index_table = jnp.zeros((EXPERTS, slot_total), jnp.int32).at[expert_of, position].set(jnp.arange(token_total, dtype=jnp.int32))
    counts = jnp.sum(onehot, axis=0)
    valid_table = jnp.arange(slot_total, dtype=jnp.int32)[None, :] < counts[:, None]
    scaled = (router_weight[:, None] * cotangent.astype(jnp.float32)).astype(jnp.bfloat16)

    def per_expert(items):
        token_index, is_valid, gate_up_slab, down_slab = items
        return expert_math((token_index, is_valid, gate_up_slab, down_slab, tokens, scaled))

    outputs, row_grads, weight_grads, down_grads = lax.map(per_expert, (index_table, valid_table, gate_up_weight, down_weight))
    out_tok = outputs[expert_of, position]
    grad_tokens = row_grads[expert_of, position]
    layer_out = (router_weight[:, None] * out_tok.astype(jnp.float32)).astype(jnp.bfloat16)
    return layer_out, grad_tokens, weight_grads, down_grads
```

```python
import jax
import jax.numpy as jnp
from jax import lax
from jax.sharding import Mesh, PartitionSpec as P

NX = 4
NZ = 4
TOKEN_AXES = ("zl", "y", "core")


def slots_of(expert_of, width, room):
    count = expert_of.shape[0]
    index = jnp.arange(count, dtype=jnp.int32)
    earlier = (expert_of[:, None] == expert_of[None, :]) & (index[None, :] < index[:, None])
    position = jnp.sum(earlier.astype(jnp.int32), axis=1)
    slot = expert_of * room + position
    return (slot[None, :] == jnp.arange(width, dtype=jnp.int32)[:, None]).astype(jnp.bfloat16)


def dot(a, b, dims):
    return lax.dot_general(a, b, (dims, ((), ())), preferred_element_type=jnp.float32)


def sum_blocks(blocks):
    b = [blocks[i].astype(jnp.float32) for i in range(blocks.shape[0])]
    return (b[0] + b[1]) + (b[2] + b[3])


def scatter_sum(partial):
    rows, width = partial.shape
    first = lax.all_to_all(partial.reshape(NX, rows // NX, width), "x", 0, 0, tiled=True)
    first = sum_blocks(first).astype(jnp.bfloat16)
    second = lax.all_to_all(first.reshape(NZ, rows // NX // NZ, width), "zh", 0, 0, tiled=True)
    return sum_blocks(second)


def gather_rows(part):
    return lax.all_gather(lax.all_gather(part, "zh", axis=0, tiled=True), "x", axis=0, tiled=True)


def shards(tokens, expert_of, router_weight, cotangent, gate_up_weight, down_weight):
    tok, feat = tokens.shape
    experts = 32
    room = 2 * tok // experts
    rows = experts * room
    w_gate = gate_up_weight[0, 0]
    w_up = gate_up_weight[0, 1]
    w_down = down_weight[0]
    ff = w_gate.shape[1]
    scaled = (router_weight[:, None] * cotangent.astype(jnp.float32)).astype(jnp.bfloat16)
    dispatch = slots_of(expert_of, rows, room)
    send = jnp.concatenate(
        [dot(dispatch, tokens, ((1,), (0,))), dot(dispatch, scaled, ((1,), (0,)))], axis=1
    ).astype(jnp.bfloat16)
    recv = lax.all_to_all(
        send.reshape(experts, room, 2 * feat), TOKEN_AXES, 0, 0, tiled=True
    ).reshape(rows, 2 * feat)
    x_rows = recv[:, :feat]
    s_rows = recv[:, feat:]

    partial = jnp.concatenate(
        [
            dot(x_rows, w_gate, ((1,), (0,))).astype(jnp.bfloat16),
            dot(x_rows, w_up, ((1,), (0,))).astype(jnp.bfloat16),
            dot(s_rows, w_down, ((1,), (1,))).astype(jnp.bfloat16),
        ],
        axis=1,
    )
    total = scatter_sum(partial)
    gate = total[:, :ff]
    up = total[:, ff : 2 * ff]
    hidden_grad = total[:, 2 * ff :]
    sig = jax.nn.sigmoid(gate)
    act = gate * sig
    part = jnp.concatenate(
        [
            act * up,
            hidden_grad * up * sig * (1.0 + gate * (1.0 - sig)),
            hidden_grad * act,
        ],
        axis=1,
    ).astype(jnp.bfloat16)
    full = gather_rows(part)
    hidden = full[:, :ff]
    gate_grad = full[:, ff : 2 * ff]
    up_grad = full[:, 2 * ff :]

    expert_out = dot(hidden, w_down, ((1,), (0,)))
    row_grad = dot(gate_grad, w_gate, ((1,), (1,))) + dot(up_grad, w_up, ((1,), (1,)))
    back = jnp.concatenate([expert_out, row_grad], axis=1).astype(jnp.bfloat16)
    back = lax.all_to_all(
        back.reshape(experts, room, 2 * feat), TOKEN_AXES, 0, 0, tiled=True
    ).reshape(rows, 2 * feat)
    grad_gate = dot(x_rows, gate_grad, ((0,), (0,)))
    grad_up = dot(x_rows, up_grad, ((0,), (0,)))
    grad_down = dot(hidden, s_rows, ((0,), (0,)))
    out = dot(dispatch, back, ((0,), (0,)))
    layer_out = (router_weight[:, None] * out[:, :feat]).astype(jnp.bfloat16)
    grad_tokens = out[:, feat:].astype(jnp.bfloat16)
    return (
        layer_out,
        grad_tokens,
        jnp.stack([grad_gate, grad_up]).astype(jnp.bfloat16)[None],
        grad_down.astype(jnp.bfloat16)[None],
    )


def solution(mesh):
    fine = Mesh(mesh.devices.reshape(NZ, NX, 2, 8, 2), ("zh", "x", "zl", "y", "core"))
    dp = ("zh", "x")
    ex = TOKEN_AXES
    return jax.shard_map(
        shards,
        mesh=fine,
        in_specs=(P(ex, dp), P(ex), P(ex), P(ex, dp), P(ex, None, dp, None), P(ex, None, dp)),
        out_specs=(P(ex, dp), P(ex, dp), P(ex, None, dp, None), P(ex, None, dp)),
        check_vma=False,
    )
```

```python
import jax
import jax.numpy as jnp
from jax import lax
from jax.sharding import Mesh, PartitionSpec as P

NX = 4
NZ = 4
EXPERTS = 32
TOKEN_AXES = ("zl", "y", "core")


def dot(a, b, dims):
    return lax.dot_general(a, b, (dims, ((), ())), preferred_element_type=jnp.float32)


def half(a):
    return a.astype(jnp.bfloat16)


def dispatch_rows(expert_of, room):
    index = jnp.arange(expert_of.shape[0], dtype=jnp.int32)
    earlier = (expert_of[:, None] == expert_of[None, :]) & (index[None, :] < index[:, None])
    base = expert_of * (2 * room) + jnp.sum(earlier.astype(jnp.int32), axis=1)
    slot = jnp.concatenate([base, base + room])
    rows = jnp.arange(EXPERTS * 2 * room, dtype=jnp.int32)
    return half(slot[None, :] == rows[:, None])


def kind_rows(room):
    rows = jnp.arange(EXPERTS * 2 * room, dtype=jnp.int32)
    kind = rows // (EXPERTS * room)
    expert = (rows // room) % EXPERTS
    column = expert * (2 * room) + kind * room + rows % room
    return half(column[:, None] == rows[None, :])


def exchange(values, axes, parts):
    rows, width = values.shape
    return lax.all_to_all(values.reshape(parts, rows // parts, width), axes, 0, 0, tiled=True)


def add_up(blocks):
    b = [blocks[i].astype(jnp.float32) for i in range(blocks.shape[0])]
    return (b[0] + b[1]) + (b[2] + b[3])


def scatter_sum(partial):
    first = half(add_up(exchange(partial, "x", NX)))
    return add_up(exchange(first, "zh", NZ))


def gather_rows(piece):
    wide = lax.all_gather(piece, "zh", axis=0, tiled=True)
    part, width = wide.shape
    copies = jnp.broadcast_to(wide[None], (NX, part, width))
    return lax.all_to_all(copies, "x", 0, 0, tiled=True).reshape(NX * part, width)


def shards(tokens, expert_of, router_weight, cotangent, gate_up_weight, down_weight):
    tok, feat = tokens.shape
    room = 2 * tok // EXPERTS
    rows = EXPERTS * room
    w_gate = gate_up_weight[0, 0]
    w_up = gate_up_weight[0, 1]
    w_down = down_weight[0]
    ff = w_gate.shape[1]
    scaled = half(router_weight[:, None] * cotangent.astype(jnp.float32))
    dispatch = dispatch_rows(expert_of, room)
    split = kind_rows(room)

    send = half(dot(dispatch, jnp.concatenate([tokens, scaled], axis=0), ((1,), (0,))))
    recv = exchange(send, TOKEN_AXES, EXPERTS).reshape(2 * rows, feat)
    x_rows = half(dot(split[:rows], recv, ((1,), (0,))))
    s_rows = half(dot(split[rows:], recv, ((1,), (0,))))
    total = scatter_sum(
        jnp.concatenate(
            [
                half(dot(x_rows, w_gate, ((1,), (0,)))),
                half(dot(x_rows, w_up, ((1,), (0,)))),
                half(dot(s_rows, w_down, ((1,), (1,)))),
            ],
            axis=1,
        )
    )
    gate = total[:, :ff]
    up = total[:, ff : 2 * ff]
    hidden_grad = total[:, 2 * ff :]
    sig = jax.nn.sigmoid(gate)
    act = gate * sig
    full = gather_rows(
        half(
            jnp.concatenate(
                [
                    act * up,
                    hidden_grad * up * sig * (1.0 + gate * (1.0 - sig)),
                    hidden_grad * act,
                ],
                axis=1,
            )
        )
    )
    hidden = full[:, :ff]
    gate_grad = full[:, ff : 2 * ff]
    up_grad = full[:, 2 * ff :]
    expert_out = half(dot(hidden, w_down, ((1,), (0,))))
    row_grad = half(dot(gate_grad, w_gate, ((1,), (1,))) + dot(up_grad, w_up, ((1,), (1,))))
    back = half(
        dot(split, jnp.concatenate([expert_out, row_grad], axis=0), ((0,), (0,)))
    )
    back = exchange(back, TOKEN_AXES, EXPERTS).reshape(2 * rows, feat)
    grad_gate = half(dot(x_rows, gate_grad, ((0,), (0,))))
    grad_up = half(dot(x_rows, up_grad, ((0,), (0,))))
    grad_down = half(dot(hidden, s_rows, ((0,), (0,))))
    result = dot(dispatch, back, ((0,), (0,)))
    return (
        half(router_weight[:, None] * result[:tok]),
        half(result[tok:]),
        jnp.stack([grad_gate, grad_up])[None],
        grad_down[None],
    )


def solution(mesh):
    fine = Mesh(mesh.devices.reshape(NZ, NX, 2, 8, 2), ("zh", "x", "zl", "y", "core"))
    dp = ("zh", "x")
    ex = TOKEN_AXES
    return jax.shard_map(
        shards,
        mesh=fine,
        in_specs=(P(ex, dp), P(ex), P(ex), P(ex, dp), P(ex, None, dp, None), P(ex, None, dp)),
        out_specs=(P(ex, dp), P(ex, dp), P(ex, None, dp, None), P(ex, None, dp)),
        check_vma=False,
    )
```

```python
import jax
import jax.numpy as jnp
from jax import lax
from jax.sharding import Mesh, PartitionSpec as P

NX = 4
NZ = 4
EXPERTS = 32
TOKEN_AXES = ("zl", "y", "core")


def dot(a, b, dims):
    return lax.dot_general(a, b, (dims, ((), ())), preferred_element_type=jnp.float32)


def half(a):
    return a.astype(jnp.bfloat16)


def dispatch_rows(expert_of, room):
    index = jnp.arange(expert_of.shape[0], dtype=jnp.int32)
    earlier = (expert_of[:, None] == expert_of[None, :]) & (index[None, :] < index[:, None])
    base = expert_of * (2 * room) + jnp.sum(earlier.astype(jnp.int32), axis=1)
    slot = jnp.concatenate([base, base + room])
    rows = jnp.arange(EXPERTS * 2 * room, dtype=jnp.int32)
    return half(slot[None, :] == rows[:, None])


def kind_rows(room, kept):
    rows = jnp.arange(EXPERTS * 2 * kept, dtype=jnp.int32)
    kind = rows // (EXPERTS * kept)
    expert = (rows // kept) % EXPERTS
    column = expert * (2 * room) + kind * room + rows % kept
    return one_hot(column, EXPERTS * 2 * room)


def one_hot(column, width):
    return half(column[:, None] == jnp.arange(width, dtype=jnp.int32)[None, :])


def exchange(values, axes, parts):
    rows, width = values.shape
    return lax.all_to_all(values.reshape(parts, rows // parts, width), axes, 0, 0, tiled=True)


def add_up(blocks):
    b = [blocks[i].astype(jnp.float32) for i in range(blocks.shape[0])]
    return (b[0] + b[1]) + (b[2] + b[3])


def scatter_sum(partial):
    first = half(add_up(exchange(partial, "x", NX)))
    return add_up(exchange(first, "zh", NZ))


def gather_rows(piece):
    wide = lax.all_gather(piece, "zh", axis=0, tiled=True)
    part, width = wide.shape
    copies = jnp.broadcast_to(wide[None], (NX, part, width))
    return lax.all_to_all(copies, "x", 0, 0, tiled=True).reshape(NX * part, width)


def expert_rows(recv, w_gate, w_up, w_down, room, kept):
    rows = EXPERTS * kept
    ff = w_gate.shape[1]
    split = kind_rows(room, kept)
    x_rows = half(dot(split[:rows], recv, ((1,), (0,))))
    s_rows = half(dot(split[rows:], recv, ((1,), (0,))))
    total = scatter_sum(
        jnp.concatenate(
            [
                half(dot(x_rows, w_gate, ((1,), (0,)))),
                half(dot(x_rows, w_up, ((1,), (0,)))),
                half(dot(s_rows, w_down, ((1,), (1,)))),
            ],
            axis=1,
        )
    )
    gate = total[:, :ff]
    up = total[:, ff : 2 * ff]
    hidden_grad = total[:, 2 * ff :]
    sig = jax.nn.sigmoid(gate)
    act = gate * sig
    full = gather_rows(
        half(
            jnp.concatenate(
                [
                    act * up,
                    hidden_grad * up * sig * (1.0 + gate * (1.0 - sig)),
                    hidden_grad * act,
                ],
                axis=1,
            )
        )
    )
    hidden = full[:, :ff]
    gate_grad = full[:, ff : 2 * ff]
    up_grad = full[:, 2 * ff :]
    expert_out = half(dot(hidden, w_down, ((1,), (0,))))
    row_grad = half(dot(gate_grad, w_gate, ((1,), (1,))) + dot(up_grad, w_up, ((1,), (1,))))
    back = half(
        dot(split, jnp.concatenate([expert_out, row_grad], axis=0), ((0,), (0,)))
    )
    spare = ((0, EXPERTS * (room - kept)), (0, 0))
    return back, jnp.pad(x_rows, spare), jnp.pad(s_rows, spare), jnp.pad(full, spare)


def shards(tokens, expert_of, router_weight, cotangent, gate_up_weight, down_weight):
    tok, feat = tokens.shape
    room = 2 * tok // EXPERTS
    rows = EXPERTS * room
    w_gate = gate_up_weight[0, 0]
    w_up = gate_up_weight[0, 1]
    w_down = down_weight[0]
    scaled = half(router_weight[:, None] * cotangent.astype(jnp.float32))
    dispatch = dispatch_rows(expert_of, room)
    send = half(dot(dispatch, jnp.concatenate([tokens, scaled], axis=0), ((1,), (0,))))
    recv = exchange(send, TOKEN_AXES, EXPERTS).reshape(2 * rows, feat)
    mine = lax.axis_index(TOKEN_AXES).astype(jnp.int32)
    busy = jnp.sum((expert_of == mine).astype(jnp.int32)) > 9
    back, x_rows, s_rows, full = lax.cond(
        busy,
        lambda *a: expert_rows(*a, room, room),
        lambda *a: expert_rows(*a, room, 9),
        recv, w_gate, w_up, w_down,
    )
    back = exchange(back, TOKEN_AXES, EXPERTS).reshape(2 * rows, feat)
    ff = w_gate.shape[1]
    grad_gate = half(dot(x_rows, full[:, ff : 2 * ff], ((0,), (0,))))
    grad_up = half(dot(x_rows, full[:, 2 * ff :], ((0,), (0,))))
    grad_down = half(dot(full[:, :ff], s_rows, ((0,), (0,))))
    result = dot(dispatch, back, ((0,), (0,)))
    return (
        half(router_weight[:, None] * result[:tok]),
        half(result[tok:]),
        jnp.stack([grad_gate, grad_up])[None],
        grad_down[None],
    )


def solution(mesh):
    fine = Mesh(mesh.devices.reshape(NZ, NX, 2, 8, 2), ("zh", "x", "zl", "y", "core"))
    dp = ("zh", "x")
    ex = TOKEN_AXES
    return jax.shard_map(
        shards,
        mesh=fine,
        in_specs=(P(ex, dp), P(ex), P(ex), P(ex, dp), P(ex, None, dp, None), P(ex, None, dp)),
        out_specs=(P(ex, dp), P(ex, dp), P(ex, None, dp, None), P(ex, None, dp)),
        check_vma=False,
    )
```

```python
import jax
import jax.numpy as jnp
from jax import lax
from jax.experimental import pallas as pl
from jax.experimental.pallas import tpu as pltpu
from jax.sharding import Mesh, PartitionSpec as P

NX = 4
NZ = 4
EXPERTS = 32
TOKEN_AXES = ("zl", "y", "core")
VMEM_BYTES = 56 * 1024 * 1024


def dot(a, b, dims):
    return lax.dot_general(a, b, (dims, ((), ())), preferred_element_type=jnp.float32)


def half(a):
    return a.astype(jnp.bfloat16)


def kernel_call(body, outs, *args):
    whole = pl.BlockSpec(memory_space=pltpu.VMEM)
    return pl.pallas_call(
        body,
        out_shape=[jax.ShapeDtypeStruct(shape, dtype) for shape, dtype in outs],
        in_specs=[whole] * len(args),
        out_specs=[whole] * len(outs),
        compiler_params=pltpu.CompilerParams(vmem_limit_bytes=VMEM_BYTES),
    )(*args)


def as_column(row):
    n = row.shape[1]
    eye = lax.broadcasted_iota(jnp.int32, (n, n), 0) == lax.broadcasted_iota(jnp.int32, (n, n), 1)
    return jnp.sum(jnp.where(eye, row, 0.0), axis=1, keepdims=True)


def where_one(mask):
    return half(jnp.where(mask, 1.0, 0.0))


def iota(shape, dim):
    return lax.broadcasted_iota(jnp.int32, shape, dim)


COUNT_LANES = 128
MAIN = 8
REST = 4
BLOCK_ROWS = EXPERTS * MAIN


def send_body(expert_ref, weight_ref, tokens_ref, cotangent_ref, send_ref):
    expert = expert_ref[...].astype(jnp.float32)
    n = expert.shape[1]
    feat = tokens_ref.shape[1]
    column = as_column(expert)
    same = (column == expert) & (iota((n, n), 0) < iota((n, n), 1))
    position = jnp.sum(jnp.where(same, 1.0, 0.0), axis=0, keepdims=True)
    slot = (expert * MAIN + position).astype(jnp.int32)
    main = jnp.where(position < MAIN, slot, -1)
    rest = jnp.where(position < MAIN, -MAIN, slot - MAIN)
    rows = iota((BLOCK_ROWS, n), 0)
    scaled = half(as_column(weight_ref[...]) * cotangent_ref[...].astype(jnp.float32))
    tokens = tokens_ref[...]
    pick = where_one(rows == main)
    send_ref[:, :feat] = half(dot(pick, tokens, ((1,), (0,))))
    send_ref[:, feat : 2 * feat] = half(dot(pick, scaled, ((1,), (0,))))
    named = jnp.where(jnp.right_shift(rows, 3) == expert_ref[...], 1.0, 0.0)
    counts = jnp.sum(named, axis=1, keepdims=True)
    send_ref[:, 3 * feat :] = half(jnp.broadcast_to(counts, (BLOCK_ROWS, COUNT_LANES)))
    send_ref[:, 2 * feat : 3 * feat] = half(
        dot(where_one(rows == rest), tokens, ((1,), (0,)))
        + dot(where_one(rows == rest + REST), scaled, ((1,), (0,)))
    )


def result_body(expert_ref, weight_ref, back_ref, out_ref, grad_ref):
    expert = expert_ref[...].astype(jnp.float32)
    n = expert.shape[1]
    feat = out_ref.shape[1]
    column = as_column(expert)
    same = (column == expert) & (iota((n, n), 1) < iota((n, n), 0))
    position = jnp.sum(jnp.where(same, 1.0, 0.0), axis=1, keepdims=True)
    slot = (column * MAIN + position).astype(jnp.int32)
    main = jnp.where(position < MAIN, slot, -1)
    rest = jnp.where(position < MAIN, -MAIN, slot - MAIN)
    columns = iota((n, BLOCK_ROWS), 1)
    pick = where_one(columns == main)
    last = back_ref[:, 2 * feat :]
    out = dot(pick, back_ref[:, :feat], ((1,), (0,))) + dot(
        where_one(columns == rest), last, ((1,), (0,))
    )
    grad = dot(pick, back_ref[:, feat : 2 * feat], ((1,), (0,))) + dot(
        where_one(columns == rest + REST), last, ((1,), (0,))
    )
    out_ref[...] = half(as_column(weight_ref[...]) * out)
    grad_ref[...] = half(grad)


def row_targets(counts):
    n = BLOCK_ROWS
    above = iota((n, n), 0)
    across = iota((n, n), 1)
    count = jnp.sum(jnp.where(above == across, counts, 0.0), axis=0, keepdims=True)
    earlier = jnp.right_shift(above, 3) < jnp.right_shift(across, 3)
    heads = (jnp.bitwise_and(above, MAIN - 1) == 0) & earlier
    offset = jnp.sum(jnp.where(heads, counts, 0.0), axis=0, keepdims=True)
    count = count.astype(jnp.int32)
    offset = offset.astype(jnp.int32)
    lane = jnp.bitwise_and(iota((1, n), 1), MAIN - 1)
    tail = MAIN + jnp.bitwise_and(lane, REST - 1)
    held = tail < count
    return (
        jnp.where(lane < count, offset + lane, -1),
        jnp.where(held & (lane < REST), offset + tail, -1),
        jnp.where(held & (lane >= REST), offset + tail, -1),
    )


def partial_body(recv_ref, w_gu_ref, w_down_ref, x_ref, s_ref, target_ref, partial_ref):
    part = partial_ref.shape[2]
    rows = NX * part
    room = x_ref.shape[0] // NX
    feat = x_ref.shape[1]
    quarter = w_down_ref.shape[0] // NZ
    index = iota((rows, BLOCK_ROWS), 0)
    targets = row_targets(recv_ref[:, 3 * feat : 3 * feat + 1].astype(jnp.float32))
    for k in range(3):
        target_ref[k : k + 1, :] = targets[k]
    pick = where_one(index == targets[0])
    last = recv_ref[:, 2 * feat : 3 * feat]
    x_rows = half(
        dot(pick, recv_ref[:, :feat], ((1,), (0,)))
        + dot(where_one(index == targets[1]), last, ((1,), (0,)))
    )
    s_rows = half(
        dot(pick, recv_ref[:, feat : 2 * feat], ((1,), (0,)))
        + dot(where_one(index == targets[2]), last, ((1,), (0,)))
    )
    for ref, values in ((x_ref, x_rows), (s_ref, s_rows)):
        for x in range(NX):
            ref[x * room : x * room + part, :] = values[x * part : (x + 1) * part]
            if part < room:
                ref[x * room + part : (x + 1) * room, :] = jnp.zeros(
                    (room - part, feat), values.dtype
                )
    for q in range(NZ):
        cols = slice(q * quarter, (q + 1) * quarter)
        products = (
            dot(x_rows, w_gu_ref[0, 0, :, cols], ((1,), (0,))),
            dot(x_rows, w_gu_ref[0, 1, :, cols], ((1,), (0,))),
            dot(s_rows, w_down_ref[cols, :], ((1,), (1,))),
        )
        for k, product in enumerate(products):
            for x in range(NX):
                partial_ref[x, q, :, k * quarter : (k + 1) * quarter] = half(
                    product[x * part : (x + 1) * part]
                )


def back_body(full_ref, target_ref, w_gu_ref, w_down_ref, back_ref, *padded_refs):
    part = full_ref.shape[2]
    rows = NX * part
    quarter = w_down_ref.shape[0] // NZ
    feat = w_down_ref.shape[1]
    out = jnp.zeros((rows, feat), jnp.float32)
    grad = jnp.zeros((rows, feat), jnp.float32)
    for q in range(NZ):
        cols = slice(q * quarter, (q + 1) * quarter)

        def values(k):
            return full_ref[:, q, :, k * quarter : (k + 1) * quarter].reshape(rows, quarter)

        out += dot(values(0), w_down_ref[cols, :], ((1,), (0,)))
        grad += dot(values(1), w_gu_ref[0, 0, :, cols], ((1,), (1,)))
        grad += dot(values(2), w_gu_ref[0, 1, :, cols], ((1,), (1,)))
    out = half(out)
    grad = half(grad)
    index = iota((rows, BLOCK_ROWS), 0)
    pick = where_one(index == target_ref[0:1, :])
    back_ref[:, :feat] = half(dot(pick, out, ((0,), (0,))))
    back_ref[:, feat : 2 * feat] = half(dot(pick, grad, ((0,), (0,))))
    back_ref[:, 2 * feat :] = half(
        dot(where_one(index == target_ref[1:2, :]), out, ((0,), (0,)))
        + dot(where_one(index == target_ref[2:3, :]), grad, ((0,), (0,)))
    )
    for ref in padded_refs:
        ref[:, :, :part, :] = full_ref[...]
        room = ref.shape[2]
        ref[:, :, part:, :] = jnp.zeros(ref.shape[:2] + (room - part, ref.shape[3]), ref.dtype)


def add_up(blocks):
    b = [blocks[i].astype(jnp.float32) for i in range(blocks.shape[0])]
    return (b[0] + b[1]) + (b[2] + b[3])


LEVELS = (192, 224, 288, 384)


def expert_rows(recv, w_gu, w_down, rows):
    full_rows = LEVELS[-1]
    part = rows // NX
    ff, feat = w_down.shape
    quarter = ff // NZ
    bf = jnp.bfloat16
    x_rows, s_rows, target, partial = kernel_call(
        partial_body,
        [
            ((full_rows, feat), bf),
            ((full_rows, feat), bf),
            ((3, BLOCK_ROWS), jnp.int32),
            ((NX, NZ, part, 3 * quarter), bf),
        ],
        recv, w_gu, w_down,
    )
    first = half(add_up(lax.all_to_all(partial, "x", 0, 0, tiled=True)))
    total = add_up(lax.all_to_all(first, "zh", 0, 0, tiled=True))
    gate = total[:, :quarter]
    up = total[:, quarter : 2 * quarter]
    hidden_grad = total[:, 2 * quarter :]
    sig = jax.nn.sigmoid(gate)
    act = gate * sig
    piece = half(
        jnp.concatenate(
            [
                act * up,
                hidden_grad * up * sig * (1.0 + gate * (1.0 - sig)),
                hidden_grad * act,
            ],
            axis=1,
        )
    )
    wide = lax.all_gather(piece, "zh", axis=0, tiled=True)
    copies = jnp.broadcast_to(
        wide.reshape(1, NZ, part, 3 * quarter), (NX, NZ, part, 3 * quarter)
    )
    full = lax.all_to_all(copies, "x", 0, 0, tiled=True)
    outs = [((BLOCK_ROWS, 3 * feat), bf)]
    if rows < full_rows:
        outs.append(((NX, NZ, full_rows // NX, 3 * quarter), bf))
    back = kernel_call(back_body, outs, full, target, w_gu, w_down)
    return back[0], x_rows, s_rows, back[-1] if rows < full_rows else full


def shards(tokens, expert_of, router_weight, cotangent, gate_up_weight, down_weight):
    tok, feat = tokens.shape
    rows = LEVELS[-1]
    w_down = down_weight[0]
    ff = w_down.shape[0]
    quarter = ff // NZ
    expert_row = expert_of.reshape(1, tok)
    weight_row = router_weight.reshape(1, tok)
    bf = jnp.bfloat16
    (send,) = kernel_call(
        send_body, [((BLOCK_ROWS, 3 * feat + COUNT_LANES), bf)], expert_row, weight_row, tokens, cotangent
    )

    def exchange(values):
        return lax.all_to_all(
            values.reshape(EXPERTS, MAIN, values.shape[1]), TOKEN_AXES, 0, 0, tiled=True
        ).reshape(values.shape)

    recv = exchange(send)
    count = jnp.sum(recv[:, 3 * feat :].astype(jnp.float32)) / (MAIN * COUNT_LANES)
    level = sum((count > limit).astype(jnp.int32) for limit in LEVELS[:-1])
    back, x_rows, s_rows, full = lax.switch(
        level,
        [lambda *a, n=n: expert_rows(*a, n) for n in LEVELS],
        recv, gate_up_weight, w_down,
    )
    back = exchange(back)
    x_parts = x_rows.reshape(NX, rows // NX, feat)
    s_parts = s_rows.reshape(NX, rows // NX, feat)
    grad_gate_up = jnp.einsum(
        "xrd,xqrf->dqf", x_parts, full[..., quarter:], preferred_element_type=jnp.float32
    )
    grad_down = jnp.einsum(
        "xqrf,xrd->qfd", full[..., :quarter], s_parts, preferred_element_type=jnp.float32
    )
    grad_gate = half(grad_gate_up[..., :quarter]).reshape(feat, ff)
    grad_up = half(grad_gate_up[..., quarter:]).reshape(feat, ff)
    layer_out, grad_tokens = kernel_call(
        result_body,
        [((tok, feat), bf), ((tok, feat), bf)],
        expert_row, weight_row, back,
    )
    return (
        layer_out,
        grad_tokens,
        jnp.stack([grad_gate, grad_up])[None],
        half(grad_down).reshape(1, ff, feat),
    )


def solution(mesh):
    fine = Mesh(mesh.devices.reshape(NZ, NX, 2, 8, 2), ("zh", "x", "zl", "y", "core"))
    dp = ("zh", "x")
    ex = TOKEN_AXES
    return jax.shard_map(
        shards,
        mesh=fine,
        in_specs=(P(ex, dp), P(ex), P(ex), P(ex, dp), P(ex, None, dp, None), P(ex, None, dp)),
        out_specs=(P(ex, dp), P(ex, dp), P(ex, None, dp, None), P(ex, None, dp)),
        check_vma=False,
    )
```

```python
import jax
import jax.numpy as jnp
import numpy as np
from jax import lax
from jax.experimental import pallas as pl
from jax.experimental.pallas import tpu as pltpu
from jax.sharding import Mesh, PartitionSpec as P

NX = 4
NZ = 4
EXPERTS = 32
TOKEN_AXES = ("zl", "y", "core")
SMALL_GRANT = 20 * 1024 * 1024
LARGE_GRANT = 56 * 1024 * 1024


def dot(a, b, dims):
    return lax.dot_general(a, b, (dims, ((), ())), preferred_element_type=jnp.float32)


def half(a):
    return a.astype(jnp.bfloat16)


def kernel_call(body, outs, *args, grant=SMALL_GRANT):
    whole = pl.BlockSpec(memory_space=pltpu.VMEM)
    return pl.pallas_call(
        body,
        out_shape=[jax.ShapeDtypeStruct(shape, dtype) for shape, dtype in outs],
        in_specs=[whole] * len(args),
        out_specs=[whole] * len(outs),
        compiler_params=pltpu.CompilerParams(vmem_limit_bytes=grant),
    )(*args)


def as_column(row):
    n = row.shape[1]
    eye = lax.broadcasted_iota(jnp.int32, (n, n), 0) == lax.broadcasted_iota(jnp.int32, (n, n), 1)
    return jnp.sum(jnp.where(eye, row, 0.0), axis=1, keepdims=True)


def where_one(mask):
    return half(jnp.where(mask, 1.0, 0.0))


def iota(shape, dim):
    return lax.broadcasted_iota(jnp.int32, shape, dim)


MOST = 9
COUNT_ROW = 3
MAIN = 8
REST = 4
BLOCK_ROWS = EXPERTS * MAIN


def send_body(expert_ref, weight_ref, tokens_ref, cotangent_ref, send_ref):
    expert = expert_ref[...].astype(jnp.float32)
    n = expert.shape[1]
    feat = tokens_ref.shape[1]
    column = as_column(expert)
    same = (column == expert) & (iota((n, n), 0) < iota((n, n), 1))
    position = jnp.sum(jnp.where(same, 1.0, 0.0), axis=0, keepdims=True)
    slot = (expert * MAIN + position).astype(jnp.int32)
    main = jnp.where(position < MAIN, slot, -1)
    rest = jnp.where(position < MAIN, -MAIN, slot - MAIN)
    rows = iota((BLOCK_ROWS, n), 0)
    scaled = half(as_column(weight_ref[...]) * cotangent_ref[...].astype(jnp.float32))
    tokens = tokens_ref[...]
    pick = where_one(rows == main)
    send_ref[:, :feat] = half(dot(pick, tokens, ((1,), (0,))))
    send_ref[:, feat : 2 * feat] = half(dot(pick, scaled, ((1,), (0,))))
    named = jnp.where(jnp.right_shift(rows, 3) == expert_ref[...], 1.0, 0.0)
    counts = jnp.sum(named, axis=1, keepdims=True)
    note = (jnp.bitwise_and(iota((BLOCK_ROWS, 1), 0), MAIN - 1) == COUNT_ROW) & (counts <= MOST)
    send_ref[:, 2 * feat :] = half(
        dot(where_one(rows == rest), tokens, ((1,), (0,)))
        + dot(where_one(rows == rest + REST), scaled, ((1,), (0,)))
        + jnp.where(note, counts, 0.0)
    )


def result_body(expert_ref, weight_ref, back_ref, out_ref, grad_ref):
    expert = expert_ref[...].astype(jnp.float32)
    n = expert.shape[1]
    feat = out_ref.shape[1]
    column = as_column(expert)
    same = (column == expert) & (iota((n, n), 1) < iota((n, n), 0))
    position = jnp.sum(jnp.where(same, 1.0, 0.0), axis=1, keepdims=True)
    slot = (column * MAIN + position).astype(jnp.int32)
    main = jnp.where(position < MAIN, slot, -1)
    rest = jnp.where(position < MAIN, -MAIN, slot - MAIN)
    columns = iota((n, BLOCK_ROWS), 1)
    pick = where_one(columns == main)
    last = back_ref[:, 2 * feat :]
    out = dot(pick, back_ref[:, :feat], ((1,), (0,))) + dot(
        where_one(columns == rest), last, ((1,), (0,))
    )
    grad = dot(pick, back_ref[:, feat : 2 * feat], ((1,), (0,))) + dot(
        where_one(columns == rest + REST), last, ((1,), (0,))
    )
    out_ref[...] = half(as_column(weight_ref[...]) * out)
    grad_ref[...] = half(grad)


def count_sums():
    i = np.arange(BLOCK_ROWS)[:, None]
    j = np.arange(BLOCK_ROWS)[None, :]
    noted = i % MAIN == COUNT_ROW
    same = noted & (i // MAIN == j // MAIN)
    earlier = noted & (i // MAIN < j // MAIN)
    return jnp.asarray(np.concatenate([same, earlier], axis=1), jnp.bfloat16)


def row_targets(notes, sums):
    n = BLOCK_ROWS
    lane = iota((1, n), 1)
    if sums is None:
        count = jnp.full((1, n), MAIN + REST, jnp.int32)
        offset = jnp.right_shift(lane, 3) * (MAIN + REST)
    else:
        both = dot(notes, sums, ((0,), (0,)))[0:1].astype(jnp.int32)
        count = both[:, :n]
        offset = both[:, n:]
    lane = jnp.bitwise_and(lane, MAIN - 1)
    tail = MAIN + jnp.bitwise_and(lane, REST - 1)
    held = tail < count
    return (
        jnp.where(lane < count, offset + lane, -1),
        jnp.where(held & (lane < REST), offset + tail, -1),
        jnp.where(held & (lane >= REST), offset + tail, -1),
    )


def partial_body(recv_ref, w_gu_ref, w_down_ref, *refs):
    *sums_ref, x_ref, s_ref, target_ref, partial_ref = refs
    part = partial_ref.shape[2]
    rows = NX * part
    room = x_ref.shape[0] // NX
    feat = x_ref.shape[1]
    quarter = w_down_ref.shape[0] // NZ
    index = iota((rows, BLOCK_ROWS), 0)
    targets = row_targets(
        recv_ref[:, 2 * feat : 2 * feat + 128], sums_ref[0][...] if sums_ref else None
    )
    for k in range(3):
        target_ref[k : k + 1, :] = targets[k]
    pick = where_one(index == targets[0])
    last = recv_ref[:, 2 * feat : 3 * feat]
    x_rows = half(
        dot(pick, recv_ref[:, :feat], ((1,), (0,)))
        + dot(where_one(index == targets[1]), last, ((1,), (0,)))
    )
    s_rows = half(
        dot(pick, recv_ref[:, feat : 2 * feat], ((1,), (0,)))
        + dot(where_one(index == targets[2]), last, ((1,), (0,)))
    )
    for ref, values in ((x_ref, x_rows), (s_ref, s_rows)):
        for x in range(NX):
            ref[x * room : x * room + part, :] = values[x * part : (x + 1) * part]
            if part < room:
                ref[x * room + part : (x + 1) * room, :] = jnp.zeros(
                    (room - part, feat), values.dtype
                )
    for q in range(NZ):
        cols = slice(q * quarter, (q + 1) * quarter)
        products = (
            dot(x_rows, w_gu_ref[0, 0, :, cols], ((1,), (0,))),
            dot(x_rows, w_gu_ref[0, 1, :, cols], ((1,), (0,))),
            dot(s_rows, w_down_ref[cols, :], ((1,), (1,))),
        )
        for k, product in enumerate(products):
            for x in range(NX):
                partial_ref[x, q, :, k * quarter : (k + 1) * quarter] = half(
                    product[x * part : (x + 1) * part]
                )


def back_body(full_ref, target_ref, w_gu_ref, w_down_ref, back_ref, *padded_refs):
    part = full_ref.shape[2]
    rows = NX * part
    quarter = w_down_ref.shape[0] // NZ
    feat = w_down_ref.shape[1]
    out = jnp.zeros((rows, feat), jnp.float32)
    grad = jnp.zeros((rows, feat), jnp.float32)
    for q in range(NZ):
        cols = slice(q * quarter, (q + 1) * quarter)

        def values(k):
            return full_ref[:, q, :, k * quarter : (k + 1) * quarter].reshape(rows, quarter)

        out += dot(values(0), w_down_ref[cols, :], ((1,), (0,)))
        grad += dot(values(1), w_gu_ref[0, 0, :, cols], ((1,), (1,)))
        grad += dot(values(2), w_gu_ref[0, 1, :, cols], ((1,), (1,)))
    out = half(out)
    grad = half(grad)
    index = iota((rows, BLOCK_ROWS), 0)
    pick = where_one(index == target_ref[0:1, :])
    back_ref[:, :feat] = half(dot(pick, out, ((0,), (0,))))
    back_ref[:, feat : 2 * feat] = half(dot(pick, grad, ((0,), (0,))))
    back_ref[:, 2 * feat :] = half(
        dot(where_one(index == target_ref[1:2, :]), out, ((0,), (0,)))
        + dot(where_one(index == target_ref[2:3, :]), grad, ((0,), (0,)))
    )
    for ref in padded_refs:
        ref[:, :, :part, :] = full_ref[...]
        room = ref.shape[2]
        ref[:, :, part:, :] = jnp.zeros(ref.shape[:2] + (room - part, ref.shape[3]), ref.dtype)


def add_up(blocks):
    b = [blocks[i].astype(jnp.float32) for i in range(blocks.shape[0])]
    return (b[0] + b[1]) + (b[2] + b[3])


LEVELS = (192, 224, 288, 384)


def expert_rows(recv, w_gu, w_down, rows):
    full_rows = LEVELS[-1]
    part = rows // NX
    ff, feat = w_down.shape
    quarter = ff // NZ
    bf = jnp.bfloat16
    x_rows, s_rows, target, partial = kernel_call(
        partial_body,
        [
            ((full_rows, feat), bf),
            ((full_rows, feat), bf),
            ((3, BLOCK_ROWS), jnp.int32),
            ((NX, NZ, part, 3 * quarter), bf),
        ],
        recv, w_gu, w_down, *([] if rows == full_rows else [count_sums()]),
    )
    first = half(add_up(lax.all_to_all(partial, "x", 0, 0, tiled=True)))
    total = add_up(lax.all_to_all(first, "zh", 0, 0, tiled=True))
    gate = total[:, :quarter]
    up = total[:, quarter : 2 * quarter]
    hidden_grad = total[:, 2 * quarter :]
    sig = jax.nn.sigmoid(gate)
    act = gate * sig
    piece = half(
        jnp.concatenate(
            [
                act * up,
                hidden_grad * up * sig * (1.0 + gate * (1.0 - sig)),
                hidden_grad * act,
            ],
            axis=1,
        )
    )
    wide = lax.all_gather(piece, "zh", axis=0, tiled=True)
    copies = jnp.broadcast_to(
        wide.reshape(1, NZ, part, 3 * quarter), (NX, NZ, part, 3 * quarter)
    )
    full = lax.all_to_all(copies, "x", 0, 0, tiled=True)
    outs = [((BLOCK_ROWS, 3 * feat), bf)]
    if rows < full_rows:
        outs.append(((NX, NZ, full_rows // NX, 3 * quarter), bf))
    back = kernel_call(back_body, outs, full, target, w_gu, w_down)
    return back[0], x_rows, s_rows, back[-1] if rows < full_rows else full


def shards(tokens, expert_of, router_weight, cotangent, gate_up_weight, down_weight):
    tok, feat = tokens.shape
    rows = LEVELS[-1]
    w_down = down_weight[0]
    ff = w_down.shape[0]
    quarter = ff // NZ
    expert_row = expert_of.reshape(1, tok)
    weight_row = router_weight.reshape(1, tok)
    bf = jnp.bfloat16
    (send,) = kernel_call(
        send_body,
        [((BLOCK_ROWS, 3 * feat), bf)],
        expert_row, weight_row, tokens, cotangent,
        grant=LARGE_GRANT,
    )

    def exchange(values):
        return lax.all_to_all(
            values.reshape(EXPERTS, MAIN, values.shape[1]), TOKEN_AXES, 0, 0, tiled=True
        ).reshape(values.shape)

    recv = exchange(send)
    mine = lax.axis_index(TOKEN_AXES).astype(jnp.int32)
    busy = jnp.sum((expert_of == mine).astype(jnp.int32)) > MOST
    notes = recv.reshape(EXPERTS, MAIN, 3 * feat)[:, COUNT_ROW, 2 * feat : 2 * feat + 128]
    count = jnp.sum(notes.astype(jnp.float32)) / 128
    level = sum((count > limit).astype(jnp.int32) for limit in LEVELS[:-2])
    level = jnp.where(busy, len(LEVELS) - 1, level)
    back, x_rows, s_rows, full = lax.switch(
        level,
        [lambda *a, n=n: expert_rows(*a, n) for n in LEVELS],
        recv, gate_up_weight, w_down,
    )
    back = exchange(back)
    x_parts = x_rows.reshape(NX, rows // NX, feat)
    s_parts = s_rows.reshape(NX, rows // NX, feat)
    grad_gate_up = jnp.einsum(
        "xrd,xqrf->dqf", x_parts, full[..., quarter:], preferred_element_type=jnp.float32
    )
    grad_down = jnp.einsum(
        "xqrf,xrd->qfd", full[..., :quarter], s_parts, preferred_element_type=jnp.float32
    )
    grad_gate = half(grad_gate_up[..., :quarter]).reshape(feat, ff)
    grad_up = half(grad_gate_up[..., quarter:]).reshape(feat, ff)
    layer_out, grad_tokens = kernel_call(
        result_body,
        [((tok, feat), bf), ((tok, feat), bf)],
        expert_row, weight_row, back,
    )
    return (
        layer_out,
        grad_tokens,
        jnp.stack([grad_gate, grad_up])[None],
        half(grad_down).reshape(1, ff, feat),
    )


def solution(mesh):
    fine = Mesh(mesh.devices.reshape(NZ, NX, 2, 8, 2), ("zh", "x", "zl", "y", "core"))
    dp = ("zh", "x")
    ex = TOKEN_AXES
    return jax.shard_map(
        shards,
        mesh=fine,
        in_specs=(P(ex, dp), P(ex), P(ex), P(ex, dp), P(ex, None, dp, None), P(ex, None, dp)),
        out_specs=(P(ex, dp), P(ex, dp), P(ex, None, dp, None), P(ex, None, dp)),
        check_vma=False,
    )
```

```python
import jax
import jax.numpy as jnp
import numpy as np
from jax import lax
from jax.experimental import pallas as pl
from jax.experimental.pallas import tpu as pltpu
from jax.sharding import Mesh, PartitionSpec as P

NX = 4
NZ = 4
EXPERTS = 32
TOKEN_AXES = ("zl", "y", "core")
SMALL_GRANT = 20 * 1024 * 1024
LARGE_GRANT = 56 * 1024 * 1024


def dot(a, b, dims):
    return lax.dot_general(a, b, (dims, ((), ())), preferred_element_type=jnp.float32)


def half(a):
    return a.astype(jnp.bfloat16)


def kernel_call(body, outs, *args, grant=SMALL_GRANT):
    whole = pl.BlockSpec(memory_space=pltpu.VMEM)
    return pl.pallas_call(
        body,
        out_shape=[jax.ShapeDtypeStruct(shape, dtype) for shape, dtype in outs],
        in_specs=[whole] * len(args),
        out_specs=[whole] * len(outs),
        compiler_params=pltpu.CompilerParams(vmem_limit_bytes=grant),
    )(*args)


def as_column(row):
    n = row.shape[1]
    eye = lax.broadcasted_iota(jnp.int32, (n, n), 0) == lax.broadcasted_iota(jnp.int32, (n, n), 1)
    return jnp.sum(jnp.where(eye, row, 0.0), axis=1, keepdims=True)


def where_one(mask):
    return half(jnp.where(mask, 1.0, 0.0))


def iota(shape, dim):
    return lax.broadcasted_iota(jnp.int32, shape, dim)


MOST = 9
COUNT_ROW = 3
MAIN = 8
REST = 4
BLOCK_ROWS = EXPERTS * MAIN


def send_body(expert_ref, weight_ref, tokens_ref, cotangent_ref, send_ref):
    expert = expert_ref[...].astype(jnp.float32)
    n = expert.shape[1]
    feat = tokens_ref.shape[1]
    column = as_column(expert)
    same = (column == expert) & (iota((n, n), 0) < iota((n, n), 1))
    position = jnp.sum(jnp.where(same, 1.0, 0.0), axis=0, keepdims=True)
    slot = (expert * MAIN + position).astype(jnp.int32)
    main = jnp.where(position < MAIN, slot, -1)
    rest = jnp.where(position < MAIN, -MAIN, slot - MAIN)
    rows = iota((BLOCK_ROWS, n), 0)
    scaled = half(as_column(weight_ref[...]) * cotangent_ref[...].astype(jnp.float32))
    tokens = tokens_ref[...]
    pick = where_one(rows == main)
    send_ref[:, :feat] = half(dot(pick, tokens, ((1,), (0,))))
    send_ref[:, feat : 2 * feat] = half(dot(pick, scaled, ((1,), (0,))))
    named = jnp.where(jnp.right_shift(rows, 3) == expert_ref[...], 1.0, 0.0)
    counts = jnp.sum(named, axis=1, keepdims=True)
    note = (jnp.bitwise_and(iota((BLOCK_ROWS, 1), 0), MAIN - 1) == COUNT_ROW) & (counts <= MOST)
    send_ref[:, 2 * feat :] = half(
        dot(where_one(rows == rest), tokens, ((1,), (0,)))
        + dot(where_one(rows == rest + REST), scaled, ((1,), (0,)))
        + jnp.where(note, counts, 0.0)
    )


def result_body(expert_ref, weight_ref, back_ref, out_ref, grad_ref):
    expert = expert_ref[...].astype(jnp.float32)
    n = expert.shape[1]
    feat = out_ref.shape[1]
    column = as_column(expert)
    same = (column == expert) & (iota((n, n), 1) < iota((n, n), 0))
    position = jnp.sum(jnp.where(same, 1.0, 0.0), axis=1, keepdims=True)
    slot = (column * MAIN + position).astype(jnp.int32)
    main = jnp.where(position < MAIN, slot, -1)
    rest = jnp.where(position < MAIN, -MAIN, slot - MAIN)
    columns = iota((n, BLOCK_ROWS), 1)
    pick = where_one(columns == main)
    last = back_ref[:, 2 * feat :]
    out = dot(pick, back_ref[:, :feat], ((1,), (0,))) + dot(
        where_one(columns == rest), last, ((1,), (0,))
    )
    grad = dot(pick, back_ref[:, feat : 2 * feat], ((1,), (0,))) + dot(
        where_one(columns == rest + REST), last, ((1,), (0,))
    )
    out_ref[...] = half(as_column(weight_ref[...]) * out)
    grad_ref[...] = half(grad)


def count_sums():
    i = np.arange(BLOCK_ROWS)[:, None]
    j = np.arange(BLOCK_ROWS)[None, :]
    noted = i % MAIN == COUNT_ROW
    same = noted & (i // MAIN == j // MAIN)
    earlier = noted & (i // MAIN < j // MAIN)
    return jnp.asarray(np.concatenate([same, earlier], axis=1), jnp.bfloat16)


def row_targets(notes, sums):
    n = BLOCK_ROWS
    lane = iota((1, n), 1)
    if sums is None:
        count = jnp.full((1, n), MAIN + REST, jnp.int32)
        offset = jnp.right_shift(lane, 3) * (MAIN + REST)
    else:
        both = dot(notes, sums, ((0,), (0,)))[0:1].astype(jnp.int32)
        count = both[:, :n]
        offset = both[:, n:]
    lane = jnp.bitwise_and(lane, MAIN - 1)
    tail = MAIN + jnp.bitwise_and(lane, REST - 1)
    held = tail < count
    return (
        jnp.where(lane < count, offset + lane, -1),
        jnp.where(held & (lane < REST), offset + tail, -1),
        jnp.where(held & (lane >= REST), offset + tail, -1),
    )


def partial_body(recv_ref, w_gu_ref, w_down_ref, *refs):
    *sums_ref, x_ref, s_ref, target_ref, partial_ref = refs
    part = partial_ref.shape[2]
    rows = NX * part
    room = x_ref.shape[0] // NX
    feat = x_ref.shape[1]
    quarter = w_down_ref.shape[0] // NZ
    index = iota((rows, BLOCK_ROWS), 0)
    targets = row_targets(
        recv_ref[:, 2 * feat : 2 * feat + 128], sums_ref[0][...] if sums_ref else None
    )
    for k in range(3):
        target_ref[k : k + 1, :] = targets[k]
    pick = where_one(index == targets[0])
    last = recv_ref[:, 2 * feat : 3 * feat]
    x_rows = half(
        dot(pick, recv_ref[:, :feat], ((1,), (0,)))
        + dot(where_one(index == targets[1]), last, ((1,), (0,)))
    )
    s_rows = half(
        dot(pick, recv_ref[:, feat : 2 * feat], ((1,), (0,)))
        + dot(where_one(index == targets[2]), last, ((1,), (0,)))
    )
    for ref, values in ((x_ref, x_rows), (s_ref, s_rows)):
        for x in range(NX):
            ref[x * room : x * room + part, :] = values[x * part : (x + 1) * part]
            if part < room:
                ref[x * room + part : (x + 1) * room, :] = jnp.zeros(
                    (room - part, feat), values.dtype
                )
    for q in range(NZ):
        cols = slice(q * quarter, (q + 1) * quarter)
        products = (
            dot(x_rows, w_gu_ref[0, 0, :, cols], ((1,), (0,))),
            dot(x_rows, w_gu_ref[0, 1, :, cols], ((1,), (0,))),
            dot(s_rows, w_down_ref[cols, :], ((1,), (1,))),
        )
        for k, product in enumerate(products):
            for x in range(NX):
                partial_ref[x, q, :, k * quarter : (k + 1) * quarter] = half(
                    product[x * part : (x + 1) * part]
                )


def back_body(full_ref, target_ref, w_gu_ref, w_down_ref, back_ref, *padded_refs):
    part = full_ref.shape[2]
    rows = NX * part
    quarter = w_down_ref.shape[0] // NZ
    feat = w_down_ref.shape[1]
    out = jnp.zeros((rows, feat), jnp.float32)
    grad = jnp.zeros((rows, feat), jnp.float32)
    for q in range(NZ):
        cols = slice(q * quarter, (q + 1) * quarter)

        def values(k):
            return full_ref[:, q, :, k * quarter : (k + 1) * quarter].reshape(rows, quarter)

        out += dot(values(0), w_down_ref[cols, :], ((1,), (0,)))
        grad += dot(values(1), w_gu_ref[0, 0, :, cols], ((1,), (1,)))
        grad += dot(values(2), w_gu_ref[0, 1, :, cols], ((1,), (1,)))
    out = half(out)
    grad = half(grad)
    index = iota((rows, BLOCK_ROWS), 0)
    pick = where_one(index == target_ref[0:1, :])
    back_ref[:, :feat] = half(dot(pick, out, ((0,), (0,))))
    back_ref[:, feat : 2 * feat] = half(dot(pick, grad, ((0,), (0,))))
    back_ref[:, 2 * feat :] = half(
        dot(where_one(index == target_ref[1:2, :]), out, ((0,), (0,)))
        + dot(where_one(index == target_ref[2:3, :]), grad, ((0,), (0,)))
    )
    for ref in padded_refs:
        ref[:, :, :part, :] = full_ref[...]
        room = ref.shape[2]
        ref[:, :, part:, :] = jnp.zeros(ref.shape[:2] + (room - part, ref.shape[3]), ref.dtype)


def add_up(blocks):
    b = [blocks[i].astype(jnp.float32) for i in range(blocks.shape[0])]
    return (b[0] + b[1]) + (b[2] + b[3])


LEVELS = (192, 224, 288, 384)


def expert_rows(recv, w_gu, w_down, rows):
    full_rows = LEVELS[-1]
    part = rows // NX
    ff, feat = w_down.shape
    quarter = ff // NZ
    bf = jnp.bfloat16
    x_rows, s_rows, target, partial = kernel_call(
        partial_body,
        [
            ((full_rows, feat), bf),
            ((full_rows, feat), bf),
            ((3, BLOCK_ROWS), jnp.int32),
            ((NX, NZ, part, 3 * quarter), bf),
        ],
        recv, w_gu, w_down, *([] if rows == full_rows else [count_sums()]),
    )
    first = half(add_up(lax.all_to_all(partial, "x", 0, 0, tiled=True)))
    total = add_up(lax.all_to_all(first, "zh", 0, 0, tiled=True))
    gate = total[:, :quarter]
    up = total[:, quarter : 2 * quarter]
    hidden_grad = total[:, 2 * quarter :]
    sig = jax.nn.sigmoid(gate)
    act = gate * sig
    piece = half(
        jnp.concatenate(
            [
                act * up,
                hidden_grad * up * sig * (1.0 + gate * (1.0 - sig)),
                hidden_grad * act,
            ],
            axis=1,
        )
    )
    wide = lax.all_gather(piece, "zh", axis=0, tiled=True)
    copies = jnp.broadcast_to(
        wide.reshape(1, NZ, part, 3 * quarter), (NX, NZ, part, 3 * quarter)
    )
    full = lax.all_to_all(copies, "x", 0, 0, tiled=True)
    outs = [((BLOCK_ROWS, 3 * feat), bf)]
    if rows < full_rows:
        outs.append(((NX, NZ, full_rows // NX, 3 * quarter), bf))
    back = kernel_call(back_body, outs, full, target, w_gu, w_down)
    return back[0], x_rows, s_rows, back[-1] if rows < full_rows else full


def shards(tokens, expert_of, router_weight, cotangent, gate_up_weight, down_weight):
    tok, feat = tokens.shape
    rows = LEVELS[-1]
    w_down = down_weight[0]
    ff = w_down.shape[0]
    quarter = ff // NZ
    expert_row = expert_of.reshape(1, tok)
    weight_row = router_weight.reshape(1, tok)
    bf = jnp.bfloat16
    (send,) = kernel_call(
        send_body,
        [((BLOCK_ROWS, 3 * feat), bf)],
        expert_row, weight_row, tokens, cotangent,
        grant=LARGE_GRANT,
    )

    def exchange(values):
        return lax.all_to_all(
            values.reshape(EXPERTS, MAIN, values.shape[1]), TOKEN_AXES, 0, 0, tiled=True
        ).reshape(values.shape)

    recv = exchange(send)
    mine = lax.axis_index(TOKEN_AXES).astype(jnp.int32)
    busy = jnp.sum((expert_of == mine).astype(jnp.int32)) > MOST

    def other(recv, w_gu, w_down):
        notes = recv.reshape(EXPERTS, MAIN, 3 * feat)[:, COUNT_ROW, 2 * feat : 2 * feat + 128]
        count = jnp.sum(notes.astype(jnp.float32)) / 128
        level = sum((count > limit).astype(jnp.int32) for limit in LEVELS[:-2])
        return lax.switch(
            level,
            [lambda *a, n=n: expert_rows(*a, n) for n in LEVELS[:-1]],
            recv, w_gu, w_down,
        )

    back, x_rows, s_rows, full = lax.cond(
        busy,
        lambda *a: expert_rows(*a, LEVELS[-1]),
        other,
        recv, gate_up_weight, w_down,
    )
    back = exchange(back)
    x_parts = x_rows.reshape(NX, rows // NX, feat)
    s_parts = s_rows.reshape(NX, rows // NX, feat)
    grad_gate_up = jnp.einsum(
        "xrd,xqrf->dqf", x_parts, full[..., quarter:], preferred_element_type=jnp.float32
    )
    grad_down = jnp.einsum(
        "xqrf,xrd->qfd", full[..., :quarter], s_parts, preferred_element_type=jnp.float32
    )
    grad_gate = half(grad_gate_up[..., :quarter]).reshape(feat, ff)
    grad_up = half(grad_gate_up[..., quarter:]).reshape(feat, ff)
    layer_out, grad_tokens = kernel_call(
        result_body,
        [((tok, feat), bf), ((tok, feat), bf)],
        expert_row, weight_row, back,
    )
    return (
        layer_out,
        grad_tokens,
        jnp.stack([grad_gate, grad_up])[None],
        half(grad_down).reshape(1, ff, feat),
    )


def solution(mesh):
    fine = Mesh(mesh.devices.reshape(NZ, NX, 2, 8, 2), ("zh", "x", "zl", "y", "core"))
    dp = ("zh", "x")
    ex = TOKEN_AXES
    return jax.shard_map(
        shards,
        mesh=fine,
        in_specs=(P(ex, dp), P(ex), P(ex), P(ex, dp), P(ex, None, dp, None), P(ex, None, dp)),
        out_specs=(P(ex, dp), P(ex, dp), P(ex, None, dp, None), P(ex, None, dp)),
        check_vma=False,
    )
```
